256 devices in a mesh: expert: 128 (over z, y, x), dp: 2 (over core).
Axes of the slice: x: 4, y: 4, z: 8, core: 2. Of those that a mesh axis runs over, the one named last changes fastest.
Arguments:
- layer_input: bfloat16 [32768, 3584], P(('expert', 'dp')), may hold values from -6 to 6
- out_grad: bfloat16 [32768, 3584], P(('expert', 'dp')), may hold values from -6 to 6
- routes: int32 [32768, 8], P(('expert', 'dp')), may hold values from 0 to 255, as said below
- gate_values: float32 [32768, 8], P(('expert', 'dp')), may hold values from 0.1 to 1
- keep_mask: int32 [32768, 8], P(('expert', 'dp')), may hold values 0 or 1
- gate_weight: bfloat16 [3584, 49152], P('dp', 'expert'), may hold values from -0.09375 to 0.09375
- up_weight: bfloat16 [3584, 49152], P('dp', 'expert'), may hold values from -0.09375 to 0.09375
- down_transposed: bfloat16 [3584, 49152], P('dp', 'expert'), may hold values from -0.15625 to 0.15625
Outputs:
- input_grad: bfloat16 [32768, 3584], P(('expert', 'dp'))
- gate_grad: bfloat16 [3584, 49152], P('dp', 'expert')
- up_grad: bfloat16 [3584, 49152], P('dp', 'expert')
- down_grad: bfloat16 [3584, 49152], P('dp', 'expert')
The draws below stay inside these ranges and needn't reach their ends.
Inputs may be any that keep to these rules, and one draw needn't show every extreme that they name: `routes`: each token names 8 different experts. Among one device's 128 tokens no expert is named more than 5 times; on every device some expert below 32 is named exactly 5 times, and one expert below 32 is named 5 times on every device.
All inputs are finite; a program needn't handle non-finite values. No bound on the sum of `keep_mask` on one device may be relied on, other than what follows from the above.
Results may differ from the reference program's by a relative error of at most 0.0065.
Values may be sent and summed in bfloat16 or wider, within the bound.
A program may use at most 128 MiB of HBM per device.

```python
import jax
import jax.numpy as jnp
from jax import lax

D = 3584
HID = 1536
EXPERTS = 256
TOP = 8
SPLIT = 4
TOK = 128
MOST = 5
LIVE = 32
F_DEV = 384
TOKENS = 32768
N_EXPERT = 128
N_DP = 2


def route_block(block_key, hot_limit, full_expert):
    count_key, own_key, row_key, column_key = jax.random.split(block_key, 4)
    live_iota = jnp.arange(LIVE, dtype=jnp.int32)
    counts = jnp.minimum(jax.random.randint(count_key, (LIVE,), 0, hot_limit + 1, dtype=jnp.int32), MOST)
    own_full = jax.random.randint(own_key, (), 0, LIVE, dtype=jnp.int32)
    counts = jnp.where((live_iota == own_full) | (live_iota == full_expert), MOST, counts).astype(jnp.int32)
    live_ends = jnp.cumsum(counts).astype(jnp.int32)
    live_total = live_ends[LIVE - 1]
    positions = jnp.arange(TOK * TOP, dtype=jnp.int32)
    live_ids = jnp.sum((positions[:, None] >= live_ends[None, :]).astype(jnp.int32), axis=1)
    dead_ids = LIVE + (positions - live_total) * (EXPERTS - LIVE) // (TOK * TOP - live_total)
    sorted_ids = jnp.where(positions < live_total, live_ids, dead_ids).astype(jnp.int32)
    route_table = sorted_ids.reshape(TOP, TOK).T
    route_table = route_table[jax.random.permutation(row_key, TOK)]
    scores = jax.random.randint(column_key, (TOK, TOP), 0, 1 << 20, dtype=jnp.int32) * TOP + jnp.arange(TOP, dtype=jnp.int32)[None, :]
    column_order = jnp.argsort(scores, axis=1)
    return jnp.take_along_axis(route_table, column_order, axis=1).astype(jnp.int32)


def draw_routes(key, part):
    hot_limit = jax.random.randint(jax.random.fold_in(key, 11), (LIVE,), 1, 2 * MOST + 1, dtype=jnp.int32)
    full_expert = jax.random.randint(jax.random.fold_in(key, 12), (), 0, LIVE, dtype=jnp.int32)
    block_keys = jax.random.split(jax.random.fold_in(key, 13), TOKENS // TOK)
    tables = jax.vmap(lambda block_key: route_block(block_key, hot_limit, full_expert))(block_keys)
    return tables.reshape(TOKENS, TOP)


def place_ends(result, stream_key, least, largest):
    extent = result.shape
    place = [jax.random.randint(jax.random.fold_in(stream_key, axis), (), 0, extent[axis]) for axis in range(len(extent))]
    result = result.at[tuple(place)].set(least)
    longest = extent.index(max(extent))
    place[longest] = (place[longest] + 1) % extent[longest]
    return result.at[tuple(place)].set(largest)


def block_scale(key, shape, shards, low, top_value):
    loudness = 1.0
    for position, shards_of in shards:
        draws = jax.random.uniform(jax.random.fold_in(jax.random.fold_in(key, 6), position), (shards_of,), jnp.float32, low / len(shards), top_value / len(shards))
        loudness = loudness * jnp.repeat(jnp.exp(draws), shape[position] // shards_of).reshape((-1,) + (1,) * (len(shape) - 1 - position))
    return loudness


def scatter_about(rng, extent, scale, limit, cuts=(), held_as=jnp.bfloat16):
    level = block_scale(rng, extent, cuts, -0.22, 0.18) if cuts else 1.0
    drawn = jax.random.normal(rng, extent, jnp.float32) * scale * level
    return jnp.minimum(jnp.maximum(drawn, -limit), limit).astype(held_as)


def setup_inputs(seed: int = 0) -> dict:
    key_of = jax.random.split(jax.random.key(seed), 9)
    return {
        "layer_input": scatter_about(key_of[0], (TOKENS, D), 1.0, 6.0, ((0, 256),)),
        "out_grad": scatter_about(key_of[1], (TOKENS, D), 1.0, 6.0, ((0, 256),)),
        "routes": draw_routes(jax.random.fold_in(key_of[8], 71), 0),
        "gate_values": jnp.clip(0.1 + 0.9 * jax.random.uniform(key_of[3], (TOKENS, TOP), jnp.float32) ** block_scale(key_of[3], (TOKENS, TOP), ((0, 256),), -0.2, 0.2), 0.1, 1.0),
        "keep_mask": place_ends((jax.random.randint(key_of[4], (TOKENS, TOP), 0, 5) < 4).astype(jnp.int32), jax.random.fold_in(key_of[4], 1), 0, 1),
        "gate_weight": scatter_about(key_of[5], (D, LIVE * HID), D ** -0.5, 0.09375, ((0, 2), (1, 128))),
        "up_weight": scatter_about(key_of[6], (D, LIVE * HID), D ** -0.5, 0.09375, ((0, 2), (1, 128))),
        "down_transposed": scatter_about(key_of[7], (D, LIVE * HID), HID ** -0.5, 0.15625, ((0, 2), (1, 128))),
    }


def silu_parts(pre_gate):
    sigma = jax.nn.sigmoid(pre_gate)
    return pre_gate * sigma, sigma * (1.0 + pre_gate * (1.0 - sigma))


def route_tables(routes, keep_mask, live_count, slot_count):
    flat_routes = routes.reshape(-1)
    flat_keep = keep_mask.reshape(-1)
    expert_iota = jnp.arange(live_count, dtype=jnp.int32)
    chosen = ((flat_routes[:, None] == expert_iota[None, :]) & (flat_keep[:, None] == 1)).astype(jnp.int32)
    route_ranks = (jnp.cumsum(chosen, axis=0) - 1).astype(jnp.int32)
    slot_iota = jnp.arange(slot_count, dtype=jnp.int32)
    matched = chosen[:, :, None] * (route_ranks[:, :, None] == slot_iota[None, None, :]).astype(jnp.int32)
    route_iota = jnp.arange(flat_routes.shape[0], dtype=jnp.int32)
    picked = jnp.sum(matched * route_iota[:, None, None], axis=0).astype(jnp.int32)
    filled = jnp.sum(matched, axis=0).astype(jnp.int32)
    return picked.reshape(-1), filled.reshape(-1)


def expert_terms(slot_inputs, slot_grads, gate_part, up_part, down_part):
    pre_gate = jnp.dot(slot_inputs, gate_part, preferred_element_type=jnp.float32)
    pre_up = jnp.dot(slot_inputs, up_part, preferred_element_type=jnp.float32)
    activated, slope = silu_parts(pre_gate)
    hidden = (activated * pre_up).astype(jnp.bfloat16)
    hidden_grad = jnp.dot(slot_grads, down_part, preferred_element_type=jnp.float32)
    gate_side = (hidden_grad * pre_up * slope).astype(jnp.bfloat16)
    up_side = (hidden_grad * activated).astype(jnp.bfloat16)
    rows_first = (((0,), (0,)), ((), ()))
    weight_terms = (
        lax.dot_general(slot_inputs, gate_side, rows_first, preferred_element_type=jnp.float32),
        lax.dot_general(slot_inputs, up_side, rows_first, preferred_element_type=jnp.float32),
        lax.dot_general(slot_grads, hidden, rows_first, preferred_element_type=jnp.float32),
    )
    return gate_side, up_side, weight_terms


def reference(layer_input, out_grad, routes, gate_values, keep_mask, gate_weight, up_weight, down_transposed):
    blocks = N_EXPERT * N_DP
    picked, filled = jax.vmap(lambda block_routes, block_keep: route_tables(block_routes, block_keep, LIVE, MOST))(
        routes.reshape(blocks, TOK, TOP), keep_mask.reshape(blocks, TOK, TOP))
    block_start = (jnp.arange(blocks, dtype=jnp.int32) * TOK)[:, None]
    global_token = (picked // TOP + block_start).astype(jnp.int32)
    route_scale = jnp.take_along_axis(gate_values.reshape(blocks, TOK * TOP), picked, axis=1) * filled.astype(jnp.float32)
    slot_inputs = jnp.take(layer_input, global_token, axis=0) * filled.astype(layer_input.dtype)[:, :, None]
    slot_grads = (jnp.take(out_grad, global_token, axis=0).astype(jnp.float32) * route_scale[:, :, None]).astype(jnp.bfloat16)
    shaped_inputs = slot_inputs.reshape(N_EXPERT, N_DP, LIVE, MOST, D)
    shaped_grads = slot_grads.reshape(N_EXPERT, N_DP, LIVE, MOST, D)
    token_index = global_token.reshape(N_EXPERT, N_DP, LIVE, MOST)
    live_slots = filled.reshape(N_EXPERT, N_DP, LIVE, MOST).astype(jnp.float32)
    input_sum = jnp.zeros((TOKENS, D), jnp.float32)
    grad_totals = None
    for replica in range(N_DP):
        inputs_replica = shaped_inputs[:, replica]
        grads_replica = shaped_grads[:, replica]

        def one_expert(expert):
            start = expert * HID
            gate_part = lax.dynamic_slice_in_dim(gate_weight, start, HID, axis=1)
            up_part = lax.dynamic_slice_in_dim(up_weight, start, HID, axis=1)
            down_part = lax.dynamic_slice_in_dim(down_transposed, start, HID, axis=1)
            inputs_now = lax.dynamic_index_in_dim(inputs_replica, expert, axis=1, keepdims=False).reshape(-1, D)
            grads_now = lax.dynamic_index_in_dim(grads_replica, expert, axis=1, keepdims=False).reshape(-1, D)
            gate_side, up_side, weight_terms = expert_terms(inputs_now, grads_now, gate_part, up_part, down_part)
            slot_total = inputs_now.shape[0]
            pieces = jnp.einsum("smf,dmf->smd", gate_side.astype(jnp.float32).reshape(slot_total, SPLIT, F_DEV),
                                gate_part.astype(jnp.float32).reshape(D, SPLIT, F_DEV))
            pieces = pieces + jnp.einsum("smf,dmf->smd", up_side.astype(jnp.float32).reshape(slot_total, SPLIT, F_DEV),
                                         up_part.astype(jnp.float32).reshape(D, SPLIT, F_DEV))
            summed = jnp.sum(lax.optimization_barrier(pieces.astype(jnp.bfloat16)).astype(jnp.float32), axis=1)
            return summed, weight_terms

        summed, weight_terms = lax.map(one_expert, jnp.arange(LIVE, dtype=jnp.int32))
        values = jnp.transpose(summed.reshape(LIVE, N_EXPERT, MOST, D), (1, 0, 2, 3)) * live_slots[:, replica][:, :, :, None]
        input_sum = input_sum.at[token_index[:, replica].reshape(-1)].add(values.reshape(-1, D))
        rounded = tuple(lax.optimization_barrier(weight_term.astype(jnp.bfloat16)).astype(jnp.float32) for weight_term in weight_terms)
        if replica == 0:
            grad_totals = rounded
        else:
            grad_totals = tuple(first_term + second_term for first_term, second_term in zip(grad_totals, rounded))
    outputs = tuple(jnp.transpose(total_term, (1, 0, 2)).reshape(D, LIVE * HID).astype(jnp.bfloat16) for total_term in grad_totals)
    return input_sum.astype(jnp.bfloat16), outputs[0], outputs[1], outputs[2]
```

```python
import functools

import jax
import jax.numpy as jnp
from jax import lax
from jax.experimental import pallas as pl
from jax.experimental.pallas import tpu as pltpu
from jax.sharding import PartitionSpec as P

NX, NY, NZ = 4, 4, 8
NP = NY * NZ
MOST = 5
QUART = 896
MESH = pl.DeviceIdType.MESH
VMEM_CAP = 64 * 1024 * 1024 - 512 * 1024
F32 = jnp.float32
BF16 = jnp.bfloat16


def vmem():
    return pl.BlockSpec(memory_space=pltpu.VMEM)


def hbm():
    return pl.BlockSpec(memory_space=pl.ANY)


def params(**kw):
    return pltpu.CompilerParams(vmem_limit_bytes=VMEM_CAP, **kw)


def iota(shape, dim):
    return lax.broadcasted_iota(jnp.int32, shape, dim)


def by_five(v):
    return (v * 205) >> 10


def as_bf16(flag):
    return jnp.where(flag, 1.0, 0.0).astype(BF16)


def pack_kernel(routes_ref, keep_ref, gate_ref, in_ref, grad_ref, send_ref, pick_ref):
    rows, tok = pick_ref.shape
    width = in_ref.shape[1]
    row = iota((rows, tok), 0)
    expert, place = row >> 3, row & 7
    live = jnp.zeros((rows, tok), F32)
    scale = jnp.zeros((rows, tok), F32)
    for k in range(routes_ref.shape[0]):
        hit = (routes_ref[k : k + 1, :] == expert) & (keep_ref[k : k + 1, :] == 1)
        live = jnp.where(hit, 1.0, live)
        scale = jnp.where(hit, gate_ref[k : k + 1, :], scale)
    before = as_bf16(iota((tok, tok), 0) < iota((tok, tok), 1))
    rank = jnp.dot(live.astype(BF16), before, preferred_element_type=F32).astype(jnp.int32)
    alive = live > 0.5
    is_input = place < MOST
    pick_ref[...] = as_bf16(alive & is_input & (rank == place))
    main = alive & (rank == jnp.where(is_input, place, place - MOST))
    tail = alive & (rank == 3 + (place >> 2))
    main_scale = jnp.sum(jnp.where(main, scale, 0.0), axis=1, keepdims=True)
    main_scale = jnp.where(is_input[:, :1], 1.0, main_scale)
    tail_scale = jnp.sum(jnp.where(tail, scale, 0.0), axis=1, keepdims=True)
    from_input = as_bf16(main & is_input)
    from_grad = as_bf16(main & jnp.logical_not(is_input))
    total = jnp.zeros((rows, QUART), F32)
    for p in range(width // QUART):
        cols = slice(p * QUART, (p + 1) * QUART)
        got = jnp.dot(from_input, in_ref[:, cols], preferred_element_type=F32)
        got = got + jnp.dot(from_grad, grad_ref[:, cols], preferred_element_type=F32)
        send_ref[:, cols] = (got * main_scale).astype(BF16)
        piece = as_bf16(tail & ((place & 3) == p))
        total = total + jnp.dot(piece, grad_ref[:, cols], preferred_element_type=F32)
    send_ref[:, width:] = (total * tail_scale).astype(BF16)


def place_of():
    me = lax.axis_index("expert")
    x, p = lax.rem(me, NX), lax.div(me, NX)
    return x, lax.rem(p, NY), lax.div(p, NY), p


def offset_of(j):
    k = lax.div(j, NY)
    dz = lax.div(k + 1, 2) * (2 * lax.rem(k, 2) - 1)
    return lax.rem(j, NY), dz


def plane_index(y, z, dy, dz):
    return lax.rem(z + dz + NZ, NZ) * NY + lax.rem(y + dy + NY, NY)


def greet(x, y, z, p):
    dp = lax.axis_index("dp")
    barrier = pltpu.get_barrier_semaphore()
    right = (p * NX + lax.rem(x + 1, NX), dp)
    left = (p * NX + lax.rem(x + NX - 1, NX), dp)
    for other in (left, right):
        pl.semaphore_signal(barrier, inc=1, device_id=other, device_id_type=MESH)

    def one(j, carry):
        dy, dz = offset_of(j)
        q = plane_index(y, z, dy, dz)
        pl.semaphore_signal(barrier, inc=1, device_id=(q * NX + x, dp), device_id_type=MESH)
        return carry

    lax.fori_loop(1, NP, one, 0)
    pl.semaphore_wait(barrier, NP + 1)
    return left, right, dp


LAG = 4


def dispatch_kernel(
    send_ref, out_ref, own_sem, plane_send, plane_recv, ring_send, left_recv, right_recv, far_recv
):
    x, y, z, p = place_of()
    left, right, dp = greet(x, y, z, p)

    def ring_copy(src, block, j, recv, device):
        return pltpu.make_async_remote_copy(
            src_ref=src,
            dst_ref=out_ref.at[block, j],
            send_sem=ring_send,
            recv_sem=recv.at[j],
            device_id=device,
            device_id_type=MESH,
        )

    own = pltpu.make_async_copy(send_ref.at[p], out_ref.at[0, 0], own_sem)
    own.start()

    def plane_copy(j):
        dy, dz = offset_of(j)
        q = plane_index(y, z, dy, dz)
        return pltpu.make_async_remote_copy(
            src_ref=send_ref.at[q],
            dst_ref=out_ref.at[0, j],
            send_sem=plane_send,
            recv_sem=plane_recv.at[j],
            device_id=(q * NX + x, dp),
            device_id_type=MESH,
        )

    def start_plane(j, carry):
        plane_copy(j).start()
        return carry

    ring_copy(send_ref.at[p], 1, 0, left_recv, right).start()
    ring_copy(send_ref.at[p], 2, 0, right_recv, left).start()
    lax.fori_loop(1, NP, start_plane, 0)

    def relay_far(j):
        @pl.when(lax.rem(j, 2) == 0)
        def _():
            ring_copy(out_ref.at[1, j], 1, j, left_recv, right).wait_recv()
            ring_copy(out_ref.at[1, j], 3, j, far_recv, right).start()

        @pl.when(lax.rem(j, 2) == 1)
        def _():
            ring_copy(out_ref.at[2, j], 2, j, right_recv, left).wait_recv()
            ring_copy(out_ref.at[2, j], 3, j, far_recv, left).start()

    def step(j, carry):
        plane_copy(j).wait_recv()
        ring_copy(out_ref.at[0, j], 1, j, left_recv, right).start()
        ring_copy(out_ref.at[0, j], 2, j, right_recv, left).start()

        @pl.when(j >= LAG)
        def _():
            relay_far(j - LAG)

        return carry

    lax.fori_loop(1, NP, step, 0)

    def drain(j, carry):
        relay_far(j)
        return carry

    lax.fori_loop(NP - LAG, NP, drain, 0)

    def rest(j, carry):
        @pl.when(lax.rem(j, 2) == 1)
        def _():
            ring_copy(out_ref.at[1, j], 1, j, left_recv, right).wait_recv()

        @pl.when(lax.rem(j, 2) == 0)
        def _():
            ring_copy(out_ref.at[2, j], 2, j, right_recv, left).wait_recv()

        ring_copy(out_ref.at[0, j], 3, j, far_recv, right).wait_recv()
        return carry

    lax.fori_loop(0, NP, rest, 0)
    own.wait()
    pltpu.make_async_copy(
        out_ref.at[0, pl.ds(0, NP - 1)], out_ref.at[0, pl.ds(0, NP - 1)], plane_send
    ).wait()
    pltpu.make_async_copy(
        out_ref.at[pl.ds(0, 3)], out_ref.at[pl.ds(0, 3)], ring_send
    ).wait()


def expert_kernel(
    got_ref, gate_w, up_w, down_w, part_ref, gate_out, up_out, down_out,
    got, both_w, down_v, xs, ss, pre, hgrad, sides, hidden, got_sem, w_sem,
):
    group = NP * MOST
    span = NP * 8
    width = xs.shape[1]
    hid = down_v.shape[1]
    loads = [
        pltpu.make_async_copy(got_ref.at[b], got.at[b], got_sem.at[b]) for b in range(NX)
    ]
    for load in loads:
        load.start()
    w_loads = [
        pltpu.make_async_copy(gate_w, both_w.at[:, pl.ds(0, hid)], w_sem.at[0]),
        pltpu.make_async_copy(up_w, both_w.at[:, pl.ds(hid, hid)], w_sem.at[1]),
        pltpu.make_async_copy(down_w, down_v, w_sem.at[2]),
    ]
    for load in w_loads:
        load.start()

    slot, place = iota((group, span), 0), iota((group, span), 1)
    which = slot - MOST * by_five(slot)
    same = (place >> 3) == by_five(slot)
    inner = place & 7
    take_x = as_bf16(same & (inner == which))
    take_s = as_bf16(same & (inner == which + MOST))
    take_t = [
        as_bf16(same & (which >= 3) & (inner == (which - 3) * 4 + p)) for p in range(width // QUART)
    ]
    for b in range(NX):
        loads[b].wait()
        rows = slice(b * group, (b + 1) * group)
        rest = got[b, :, width:]
        for p in range(width // QUART):
            cols = slice(p * QUART, (p + 1) * QUART)
            block = got[b, :, cols]
            xs[rows, cols] = jnp.dot(take_x, block, preferred_element_type=F32).astype(BF16)
            picked = jnp.dot(take_s, block, preferred_element_type=F32)
            picked = picked + jnp.dot(take_t[p], rest, preferred_element_type=F32)
            ss[rows, cols] = picked.astype(BF16)

    w_loads[0].wait()
    w_loads[1].wait()

    @pl.loop(0, 2 * hid // 256)
    def _(n):
        cols = pl.ds(pl.multiple_of(n * 256, 256), 256)
        pre[:, cols] = jnp.dot(xs[...], both_w[:, cols], preferred_element_type=F32)

    w_loads[2].wait()
    hgrad[...] = jnp.dot(ss[...], down_v[...], preferred_element_type=F32)

    @pl.loop(0, NX * group // 64)
    def _(i):
        rows = pl.ds(pl.multiple_of(i * 64, 64), 64)
        gate, up, hg = pre[rows, :hid], pre[rows, hid:], hgrad[rows, :]
        sigma = jax.nn.sigmoid(gate)
        activated = gate * sigma
        hidden[rows, :] = (activated * up).astype(BF16)
        slope = sigma * (1.0 + gate * (1.0 - sigma))
        sides[rows, :hid] = (hg * up * slope).astype(BF16)
        sides[rows, hid:] = (hg * activated).astype(BF16)

    across = (((1,), (1,)), ((), ()))
    down = (((0,), (0,)), ((), ()))

    @pl.loop(0, width // 512)
    def _(n):
        cols = pl.ds(pl.multiple_of(n * 512, 512), 512)
        part_ref[:, cols] = lax.dot_general(
            sides[...], both_w[cols, :], across, preferred_element_type=F32
        ).astype(BF16)

    @pl.loop(0, width // 512)
    def _(n):
        cols = pl.ds(pl.multiple_of(n * 512, 512), 512)
        term = lax.dot_general(xs[:, cols], sides[...], down, preferred_element_type=F32)
        gate_out[cols, :] = term[:, :hid].astype(BF16)
        up_out[cols, :] = term[:, hid:].astype(BF16)
        term = lax.dot_general(ss[:, cols], hidden[...], down, preferred_element_type=F32)
        down_out[cols, :] = term.astype(BF16)


CH = 8
ROWS = CH * MOST
NC = NP // CH


def return_kernel(
    part_ref, ret_ref, half, pass_on, near_left, near_right, message,
    far_recv, left_recv, right_recv, ring_send, plane_send, plane_recv, own_sem,
):
    x, y, z, p = place_of()
    left, right, dp = greet(x, y, z, p)

    def ring_copy(src, dst, recv, device):
        return pltpu.make_async_remote_copy(
            src_ref=src, dst_ref=dst, send_sem=ring_send, recv_sem=recv,
            device_id=device, device_id_type=MESH,
        )

    def rows_of(block, k):
        return part_ref.at[pl.ds((block * NC + k) * ROWS, ROWS)]

    def far(k):
        return ring_copy(rows_of(3, k), half.at[k], far_recv.at[k], right if k % 2 == 0 else left)

    def direct(k):
        if k % 2 == 0:
            return ring_copy(rows_of(1, k), near_right.at[k], right_recv.at[k], left)
        return ring_copy(rows_of(2, k), near_left.at[k], left_recv.at[k], right)

    def summed(k):
        if k % 2 == 0:
            return ring_copy(pass_on.at[k], near_left.at[k], left_recv.at[k], right)
        return ring_copy(pass_on.at[k], near_right.at[k], right_recv.at[k], left)

    def plane_copy(j):
        dy, dz = offset_of(j)
        q = plane_index(y, z, -dy, -dz)
        return pltpu.make_async_remote_copy(
            src_ref=message.at[j], dst_ref=ret_ref.at[p], send_sem=plane_send, recv_sem=plane_recv,
            device_id=(q * NX + x, dp), device_id_type=MESH,
        )

    far(0).start()
    far(1).start()
    direct(0).start()
    direct(1).start()
    far(2).start()
    far(3).start()
    direct(2).start()
    direct(3).start()
    for k in range(NC):
        far(k).wait_recv()
        block = 2 if k % 2 == 0 else 1
        mine = part_ref[pl.ds((block * NC + k) * ROWS, ROWS), :].astype(F32)
        pass_on[k] = (mine + half[k].astype(F32)).astype(BF16)
        summed(k).start()
    spread_row, spread_col = iota((CH * 8, ROWS), 0), iota((CH * 8, ROWS), 1)
    spread = as_bf16(
        ((spread_row >> 3) == by_five(spread_col))
        & ((spread_row & 7) == spread_col - MOST * by_five(spread_col))
    )
    for k in range(NC):
        ring_copy(pass_on.at[k], near_left.at[k], left_recv.at[k], right).wait_recv()
        ring_copy(pass_on.at[k], near_right.at[k], right_recv.at[k], left).wait_recv()
        total = part_ref[pl.ds(k * ROWS, ROWS), :].astype(F32)
        total = total + near_left[k].astype(F32) + near_right[k].astype(F32)
        out = jnp.dot(spread, total.astype(BF16), preferred_element_type=F32).astype(BF16)
        message[pl.ds(k * CH, CH)] = out.reshape(CH, 8, out.shape[1])

        def start_plane(j, carry):
            plane_copy(j).start()
            return carry

        lax.fori_loop(max(1, k * CH), (k + 1) * CH, start_plane, 0)
        if k == 0:
            own = pltpu.make_async_copy(message.at[0], ret_ref.at[p], own_sem)
            own.start()
    own.wait()
    most = pl.ds(0, NP - 1)
    pltpu.make_async_copy(message.at[most], message.at[most], plane_recv).wait()
    pltpu.make_async_copy(message.at[most], message.at[most], plane_send).wait()
    pltpu.make_async_copy(
        part_ref.at[pl.ds(0, 3 * NC * ROWS)], part_ref.at[pl.ds(0, 3 * NC * ROWS)], ring_send
    ).wait()


def combine_kernel(pick_ref, ret_ref, out_ref):
    width = out_ref.shape[1]

    @pl.loop(0, width // 512)
    def _(n):
        cols = pl.ds(pl.multiple_of(n * 512, 512), 512)
        out_ref[:, cols] = lax.dot_general(
            pick_ref[...], ret_ref[:, cols], (((0,), (0,)), ((), ())), preferred_element_type=F32
        ).astype(BF16)


def body(layer_input, out_grad, routes, gate_values, keep_mask, gate_weight, up_weight, down_w):
    tok, width = layer_input.shape
    hid = gate_weight.shape[1]
    group = NP * MOST
    span = NP * 8
    packed = width + QUART
    dma = pltpu.SemaphoreType.DMA

    def shape(*dims, dtype=BF16):
        return jax.ShapeDtypeStruct(dims, dtype)

    weights = [
        lax.all_gather(w, "dp", axis=0, tiled=True) for w in (gate_weight, up_weight, down_w)
    ]
    send, pick = pl.pallas_call(
        pack_kernel,
        out_shape=(shape(span, packed), shape(span, tok)),
        in_specs=[vmem()] * 5,
        out_specs=(vmem(), vmem()),
        compiler_params=params(),
        name="pack",
    )(routes.T, keep_mask.T, gate_values.T, layer_input, out_grad)
    got = pl.pallas_call(
        dispatch_kernel,
        out_shape=shape(NX, NP, 8, packed),
        in_specs=[hbm()],
        out_specs=hbm(),
        scratch_shapes=[dma, dma, dma((NP,)), dma, dma((NP,)), dma((NP,)), dma((NP,))],
        compiler_params=params(collective_id=0, has_side_effects=True),
        cost_estimate=pl.CostEstimate(flops=0, bytes_accessed=300_000_000, transcendentals=0),
        name="dispatch",
    )(send.reshape(NP, 8, packed))
    parts, gate_term, up_term, down_term = pl.pallas_call(
        expert_kernel,
        out_shape=(
            shape(NX * group, width),
            shape(width, hid),
            shape(width, hid),
            shape(width, hid),
        ),
        in_specs=[hbm()] * 4,
        out_specs=(vmem(),) * 4,
        scratch_shapes=[
            pltpu.VMEM((NX, span, packed), BF16),
            pltpu.VMEM((width, 2 * hid), BF16),
            pltpu.VMEM((width, hid), BF16),
            pltpu.VMEM((NX * group, width), BF16),
            pltpu.VMEM((NX * group, width), BF16),
            pltpu.VMEM((NX * group, 2 * hid), F32),
            pltpu.VMEM((NX * group, hid), F32),
            pltpu.VMEM((NX * group, 2 * hid), BF16),
            pltpu.VMEM((NX * group, hid), BF16),
            dma((NX,)),
            dma((3,)),
        ],
        compiler_params=params(),
        name="expert",
    )(got.reshape(NX, span, packed), *weights)
    ret = pl.pallas_call(
        return_kernel,
        out_shape=shape(NP, 8, width),
        in_specs=[vmem()],
        out_specs=vmem(),
        scratch_shapes=[
            pltpu.VMEM((NC, ROWS, width), BF16),
            pltpu.VMEM((NC, ROWS, width), BF16),
            pltpu.VMEM((NC, ROWS, width), BF16),
            pltpu.VMEM((NC, ROWS, width), BF16),
            pltpu.VMEM((NP, 8, width), BF16),
            dma((NC,)),
            dma((NC,)),
            dma((NC,)),
            dma,
            dma,
            dma,
            dma,
        ],
        compiler_params=params(collective_id=1, has_side_effects=True),
        cost_estimate=pl.CostEstimate(flops=0, bytes_accessed=200_000_000, transcendentals=0),
        name="return",
    )(parts)
    input_grad = pl.pallas_call(
        combine_kernel,
        out_shape=shape(tok, width),
        in_specs=[vmem()] * 2,
        out_specs=vmem(),
        compiler_params=params(),
        name="combine",
    )(pick, ret.reshape(span, width))
    gate_grad, up_grad, down_grad = [
        lax.psum_scatter(term, "dp", scatter_dimension=0, tiled=True)
        for term in (gate_term, up_term, down_term)
    ]
    return input_grad, gate_grad, up_grad, down_grad


def solution(mesh):
    rows = P(("expert", "dp"), None)
    cols = P("dp", "expert")
    return jax.shard_map(
        body,
        mesh=mesh,
        in_specs=(rows,) * 5 + (cols,) * 3,
        out_specs=(rows, cols, cols, cols),
        check_vma=False,
    )
```
